128 devices in a mesh: lon: 16 (over z, y_hi, core), lat: 8 (over x, y_lo).
Axes of the slice: x: 4, y: 4 (y_hi: 2, y_lo: 2; y = y_hi * 2 + y_lo), z: 4, core: 2. Of those that a mesh axis runs over, the one named last changes fastest.
Arguments:
- thermal_anomaly: float32 [16, 1024, 2048], P(None, 'lat', 'lon'), may hold values from -6 to 6
- saltiness_anomaly: float32 [16, 1024, 2048], P(None, 'lat', 'lon'), may hold values from -5 to 5
- zonal_transport_ratio: float32 [16, 1024, 2048], P(None, 'lat', 'lon'), may hold values from -0.4 to 0.4
- meridional_transport_ratio: float32 [16, 1024, 2048], P(None, 'lat', 'lon'), may hold values from -0.4 to 0.4
- water_indicator: int32 [16, 1024, 2048], P(None, 'lat', 'lon'), may hold values 0 or 1
- water_layer_tally: int32 [1024, 2048], P('lat', 'lon'), may hold values from 0 to 16
Outputs:
- advanced_thermal: float32 [16, 1024, 2048], P(None, 'lat', 'lon')
- advanced_saltiness: float32 [16, 1024, 2048], P(None, 'lat', 'lon')
The draws below stay inside these ranges and needn't reach their ends.
All inputs are finite; a program needn't handle non-finite values. No bound on the sum of `water_indicator` on one device may be relied on, other than what follows from the above.
Results may differ from the reference program's by a relative error of at most 0.0003.
Values sent between devices are 32-bit elements; how exact they have to be, the bound alone decides.
A program may use at most 192 MiB of HBM per device.

```python
import jax
import jax.numpy as jnp
from jax import lax

VERTICAL_LAYERS = 16
ZONAL_SPAN = 2048
MERIDIONAL_SPAN = 1024


def with_ends(drawn, own_key, least, largest):
    index_at = [jax.random.randint(jax.random.fold_in(own_key, axis), (), 0, length) for axis, length in enumerate(drawn.shape)]
    main_axis = drawn.shape.index(max(drawn.shape))
    beside = index_at[:main_axis] + [(index_at[main_axis] + 1) % drawn.shape[main_axis]] + index_at[main_axis + 1:]
    return drawn.at[tuple(index_at)].set(least).at[tuple(beside)].set(largest)


def steps_of(key, extent, cuts, smallest, high):
    factor_of, own = 1.0, jax.random.fold_in(key, 6)
    for dim, shards_of in cuts:
        heights = jnp.exp(jax.random.uniform(jax.random.fold_in(own, dim), (shards_of,), jnp.float32, smallest / len(cuts), high / len(cuts)))
        factor_of = factor_of * jnp.repeat(heights, extent[dim] // shards_of).reshape([-1 if axis == dim else 1 for axis in range(len(extent))])
    return factor_of


def centred(stream_key, dims, deviation, bound, split=(), held_as=jnp.bfloat16):
    array = deviation * jax.random.normal(stream_key, dims, jnp.float32)
    if split:
        array = array * steps_of(stream_key, dims, split, -0.22, 0.18)
    return jnp.clip(array, -bound, bound).astype(held_as)


def setup_inputs(seed: int = 0) -> dict:
    arg_keys = jax.random.split(jax.random.key(seed), 7)
    thermal_anomaly = centred(arg_keys[0], (VERTICAL_LAYERS, MERIDIONAL_SPAN, ZONAL_SPAN), 1.0, 6.0, ((1, 8), (2, 16)), jnp.float32)
    saltiness_anomaly = centred(arg_keys[1], (VERTICAL_LAYERS, MERIDIONAL_SPAN, ZONAL_SPAN), 0.7, 5.0, ((1, 8), (2, 16)), jnp.float32)
    zonal_transport_ratio = jnp.clip(jax.random.uniform(arg_keys[2], (VERTICAL_LAYERS, MERIDIONAL_SPAN, ZONAL_SPAN), jnp.float32, -0.4, 0.4) * steps_of(arg_keys[2], (VERTICAL_LAYERS, MERIDIONAL_SPAN, ZONAL_SPAN), ((1, 8), (2, 16)), -0.4, 0.0), -0.4, 0.4)
    meridional_transport_ratio = jnp.clip(jax.random.uniform(arg_keys[3], (VERTICAL_LAYERS, MERIDIONAL_SPAN, ZONAL_SPAN), jnp.float32, -0.4, 0.4) * steps_of(arg_keys[3], (VERTICAL_LAYERS, MERIDIONAL_SPAN, ZONAL_SPAN), ((1, 8), (2, 16)), -0.4, 0.0), -0.4, 0.4)
    water_indicator = with_ends((jax.random.randint(arg_keys[4], (VERTICAL_LAYERS, MERIDIONAL_SPAN, ZONAL_SPAN), 0, 5) < 4).astype(jnp.int32), jax.random.fold_in(arg_keys[4], 1), 0, 1)
    water_layer_tally = with_ends(jax.random.randint(arg_keys[5], (MERIDIONAL_SPAN, ZONAL_SPAN), 0, VERTICAL_LAYERS + 1), jax.random.fold_in(arg_keys[5], 1), 0, VERTICAL_LAYERS).astype(jnp.int32)
    return dict(thermal_anomaly=thermal_anomaly, saltiness_anomaly=saltiness_anomaly, zonal_transport_ratio=zonal_transport_ratio, meridional_transport_ratio=meridional_transport_ratio, water_indicator=water_indicator, water_layer_tally=water_layer_tally)


DIFFUSIVITY = 0.12
LIMIT_FLOOR = 0.01


def shift_east(field):
    return jnp.roll(field, -1, axis=-1)


def shift_west(field):
    return jnp.roll(field, 1, axis=-1)


def shift_north(field):
    return jnp.concatenate([field[..., 1:, :], jnp.flip(field[..., -1:, :], axis=-1)], axis=-2)


def shift_south(field):
    return jnp.concatenate([jnp.zeros_like(field[..., :1, :]), field[..., :-1, :]], axis=-2)


def spread(flux_x, flux_y):
    return flux_x - shift_west(flux_x) + flux_y - shift_south(flux_y)


def level_step(tracers, u_level, v_level, water_site_sum):
    u_mask = water_site_sum * shift_east(water_site_sum)
    v_mask = water_site_sum * shift_north(water_site_sum)
    top_face = 0.5 * (v_level[-1:, :] - jnp.flip(v_level[-1:, :], axis=-1))
    v_face = jnp.concatenate([v_level[:-1, :], top_face], axis=0)
    q_east = shift_east(tracers)
    q_north = shift_north(tracers)
    low_x = (jnp.maximum(u_level, 0.0) * tracers + jnp.minimum(u_level, 0.0) * q_east) * u_mask
    low_y = (jnp.maximum(v_face, 0.0) * tracers + jnp.minimum(v_face, 0.0) * q_north) * v_mask
    high_x = u_level * 0.5 * (tracers + q_east) * u_mask
    high_y = v_face * 0.5 * (tracers + q_north) * v_mask
    anti_x = high_x - low_x
    anti_y = high_y - low_y
    diff_x = DIFFUSIVITY * u_mask * (q_east - tracers)
    diff_y = DIFFUSIVITY * v_mask * (q_north - tracers)
    low_order = tracers - spread(low_x, low_y)
    upper = jnp.maximum(tracers, low_order)
    lower = jnp.minimum(tracers, low_order)
    w_mask = shift_west(u_mask)
    s_mask = shift_south(v_mask)
    q_max = upper
    q_min = lower
    for face_mask, mover in ((u_mask, shift_east), (w_mask, shift_west), (v_mask, shift_north), (s_mask, shift_south)):
        q_max = jnp.maximum(q_max, jnp.where(face_mask > 0.0, mover(upper), upper))
        q_min = jnp.minimum(q_min, jnp.where(face_mask > 0.0, mover(lower), lower))
    anti_w = shift_west(anti_x)
    anti_s = shift_south(anti_y)
    inflow = jnp.maximum(anti_w, 0.0) - jnp.minimum(anti_x, 0.0) + jnp.maximum(anti_s, 0.0) - jnp.minimum(anti_y, 0.0)
    outflow = jnp.maximum(anti_x, 0.0) - jnp.minimum(anti_w, 0.0) + jnp.maximum(anti_y, 0.0) - jnp.minimum(anti_s, 0.0)
    ratio_in = jnp.minimum(1.0, (q_max - low_order) / jnp.maximum(inflow, LIMIT_FLOOR))
    ratio_out = jnp.minimum(1.0, (low_order - q_min) / jnp.maximum(outflow, LIMIT_FLOOR))
    limit_x = jnp.where(anti_x >= 0.0, jnp.minimum(shift_east(ratio_in), ratio_out), jnp.minimum(ratio_in, shift_east(ratio_out)))
    limit_y = jnp.where(anti_y >= 0.0, jnp.minimum(shift_north(ratio_in), ratio_out), jnp.minimum(ratio_in, shift_north(ratio_out)))
    return low_order - spread(limit_x * anti_x, limit_y * anti_y) + spread(diff_x, diff_y)


def reference(thermal_anomaly, saltiness_anomaly, zonal_transport_ratio, meridional_transport_ratio, water_indicator, water_layer_tally):
    layer_indices_list = jnp.arange(VERTICAL_LAYERS, dtype=jnp.int32)

    def layer_partition(level_slice):
        temp_level, salt_level, u_level, v_level, mask_level, level_id = level_slice
        water_site_sum = jnp.where((mask_level == 1) & (level_id < water_layer_tally), 1.0, 0.0).astype(jnp.float32)
        stepped = level_step(jnp.stack([temp_level, salt_level]), u_level, v_level, water_site_sum)
        return stepped[0], stepped[1]

    advanced_thermal, advanced_saltiness = lax.map(layer_partition, (thermal_anomaly, saltiness_anomaly, zonal_transport_ratio, meridional_transport_ratio, water_indicator, layer_indices_list))
    return advanced_thermal, advanced_saltiness
```

```python
import functools

import jax
import jax.numpy as jnp
from jax import lax
from jax.experimental import pallas as pl
from jax.experimental.pallas import tpu as pltpu
from jax.sharding import PartitionSpec as P

MESH = pl.DeviceIdType.MESH
DIFFUSIVITY = 0.12
LIMIT_FLOOR = 0.01
BIG = 1e30

LEVELS = 16
TILE = 128
HALO = 3
ROWS = TILE + 2 * HALO
SPAN = 18
GROUPS = 7
RUN = 20
EDGE_ROWS = RUN + 2 * HALO
LAST = GROUPS - 1
TAIL = TILE - LAST * RUN

T, S, U, V, WET = range(5)
UP, LO, AX, AY, LOW, DX, DY = range(7)


def roll(value, shift):
    return pltpu.roll(value, shift % 128, 1)


def east(value):
    return roll(value, -1)


def west(value):
    return roll(value, 1)


def flux_row(f, x, base, count):
    wet = [f[WET, base - 1 + i] for i in range(count + 2)]
    tracers = [[f[q, base - 1 + i] for i in range(count + 2)] for q in (T, S)]
    previous = [None, None]
    for i in range(count + 1):
        row = base - 1 + i
        v_mask = wet[i] * wet[i + 1]
        half_y = 0.5 * f[V, row] * v_mask
        speed_y = jnp.abs(half_y)
        mix_y = DIFFUSIVITY * v_mask
        if i > 0:
            u_mask = wet[i] * east(wet[i])
            half_x = 0.5 * f[U, row] * u_mask
            speed_x = jnp.abs(half_x)
            mix_x = DIFFUSIVITY * u_mask
            sea = wet[i] > 0.0
        for n in range(2):
            q, north = tracers[n][i], tracers[n][i + 1]
            slope_y = north - q
            anti_y = speed_y * slope_y
            low_y = half_y * (north + q) - anti_y
            if i > 0:
                right = east(q)
                slope_x = right - q
                anti_x = speed_x * slope_x
                low_x = half_x * (right + q) - anti_x
                low = q - ((low_x - west(low_x)) + (low_y - previous[n]))
                x[UP, n, row] = jnp.where(sea, jnp.maximum(q, low), -BIG)
                x[LO, n, row] = jnp.where(sea, jnp.minimum(q, low), BIG)
                x[AX, n, row] = anti_x
                x[LOW, n, row] = low
                x[DX, n, row] = mix_x * slope_x
            x[AY, n, row] = anti_y
            x[DY, n, row] = mix_y * slope_y
            previous[n] = low_y


def ratio_row(x, r, base, count):
    for n in range(2):
        anti = x[AY, n, base - 1]
        below_in, below_out = jnp.maximum(anti, 0.0), jnp.minimum(anti, 0.0)
        upper = [x[UP, n, base - 1 + i] for i in range(count + 2)]
        lower = [x[LO, n, base - 1 + i] for i in range(count + 2)]
        for i in range(count):
            row = base + i
            high, least = upper[i + 1], lower[i + 1]
            q_max = jnp.maximum(
                jnp.maximum(jnp.maximum(east(high), west(high)), high),
                jnp.maximum(upper[i], upper[i + 2]),
            )
            q_min = jnp.minimum(
                jnp.minimum(jnp.minimum(east(least), west(least)), least),
                jnp.minimum(lower[i], lower[i + 2]),
            )
            anti_x = x[AX, n, row]
            anti_w = west(anti_x)
            anti_y = x[AY, n, row]
            above_in, above_out = jnp.maximum(anti_y, 0.0), jnp.minimum(anti_y, 0.0)
            inflow = (jnp.maximum(anti_w, 0.0) - jnp.minimum(anti_x, 0.0)) + (below_in - above_out)
            outflow = (jnp.maximum(anti_x, 0.0) - jnp.minimum(anti_w, 0.0)) + (above_in - below_out)
            low = x[LOW, n, row]
            r[0, n, row] = jnp.minimum(1.0, (q_max - low) / jnp.maximum(inflow, LIMIT_FLOOR))
            r[1, n, row] = jnp.minimum(1.0, (low - q_min) / jnp.maximum(outflow, LIMIT_FLOOR))
            below_in, below_out = above_in, above_out


def final_row(x, r, base, count, emit):
    for n in range(2):
        into = [r[0, n, base - 1 + i] for i in range(count + 2)]
        out = [r[1, n, base - 1 + i] for i in range(count + 2)]
        previous = None
        for i in range(count + 1):
            row = base - 1 + i
            anti_y = x[AY, n, row]
            limit_y = jnp.where(
                anti_y >= 0.0, jnp.minimum(into[i + 1], out[i]), jnp.minimum(into[i], out[i + 1])
            )
            flux_y = limit_y * anti_y - x[DY, n, row]
            if i > 0:
                anti_x = x[AX, n, row]
                limit_x = jnp.where(
                    anti_x >= 0.0,
                    jnp.minimum(east(into[i]), out[i]),
                    jnp.minimum(into[i], east(out[i])),
                )
                flux_x = limit_x * anti_x - x[DX, n, row]
                emit(n, i - 1, x[LOW, n, row] - ((flux_x - west(flux_x)) + (flux_y - previous)))
            previous = flux_y


def mirrored(value, lane):
    for bit in (64, 32, 16, 8, 4, 2, 1):
        if bit == 64:
            value = roll(value, 64)
        else:
            value = jnp.where(lax.rem(lane // bit, 2) == 1, roll(value, bit), roll(value, -bit))
    return value


def kernel(
    lons, lats,
    t_in, s_in, u_in, v_in, ind_in, tally_in, t_out, s_out,
    nat, nat_i, nat_t, f, x, r, e, xe, re, eq, own, late,
    to_east, to_west, from_west, from_east, late_east, late_west, late_from_west, late_from_east,
    result, in_sem, out_sem, send_sem, recv_sem,
):
    lon, lat = lax.axis_index("lon"), lax.axis_index("lat")
    top = lat // (lats - 1)
    is_top, has_south = lat == lats - 1, lat > 0
    right, left = lax.rem(lon + 1, lons), lax.rem(lon + lons - 1, lons)
    north_lon = lon + top * (lons - 1 - 2 * lon)
    north_lat = lat + 1 - top

    loads = [
        pltpu.make_async_copy(src, dst, in_sem.at[i])
        for i, (src, dst) in enumerate(
            [
                (ind_in, nat_i), (tally_in, nat_t), (t_in, nat.at[T]),
                (s_in, nat.at[S]), (u_in, nat.at[U]), (v_in, nat.at[V]),
            ]
        )
    ]
    for copy in loads:
        copy.start()

    barrier = pltpu.get_barrier_semaphore()

    def greet(at_lon, at_lat):
        pl.semaphore_signal(barrier, inc=1, device_id={"lon": at_lon, "lat": at_lat}, device_id_type=MESH)

    greet(right, lat)
    greet(left, lat)
    greet(north_lon, north_lat)

    @pl.when(has_south)
    def _():
        greet(lon, lat - 1)

    lane = lax.broadcasted_iota(jnp.int32, (LEVELS, 128), 1)
    level = lax.broadcasted_iota(jnp.int32, (LEVELS, 128), 0)
    group = lane // SPAN
    slot = lane - group * SPAN

    def window(value):
        return jnp.where(lane < 6, value, roll(value, 12))

    def placed(value, at, into):
        first = at * SPAN + HALO
        return jnp.where((lane >= first) & (lane < first + 12), roll(value, first), into)

    for copy in loads:
        copy.wait()

    @pl.when(lat == 0)
    def _():
        f[:, 0:HALO] = jnp.zeros((5, HALO, LEVELS, 128), jnp.float32)

    def pack(groups, row, carry):
        acc = [jnp.zeros((LEVELS, 128), jnp.float32) for _ in range(5)]
        for g in range(groups):
            j = g * RUN + row

            def strided(ref):
                return jnp.concatenate(
                    [ref[pl.ds(j, 8, stride=TILE), :], ref[pl.ds(j + 8 * TILE, 8, stride=TILE), :]], axis=0
                )

            values = [strided(nat.at[q]) for q in range(4)]
            tally = jnp.broadcast_to(nat_t[pl.ds(j, 1), :], (LEVELS, 128))
            values.append(jnp.where((strided(nat_i) == 1) & (level < tally), 1.0, 0.0).astype(jnp.float32))
            for q in range(5):
                f[q, j + HALO] = values[q]
                acc[q] = placed(window(values[q]), g, acc[q])
        for q in range(5):
            own[q, row] = acc[q]
        return carry

    lax.fori_loop(0, TAIL, functools.partial(pack, GROUPS), 0)
    lax.fori_loop(TAIL, RUN, functools.partial(pack, GROUPS - 1), 0)

    def columns(source, row, eastward, westward):
        over, under = jnp.zeros((LEVELS, 128), jnp.float32), jnp.zeros((LEVELS, 128), jnp.float32)
        for q in range(5):
            mine = (slot >= 3 * q) & (slot < 3 * q + 3)
            value = source[q, row]
            over = jnp.where(mine, roll(value, 3 * q - 12), over)
            under = jnp.where(mine, roll(value, 3 * q - 3), under)
        eastward[row] = over
        westward[row] = under

    def columns_loop(row, carry):
        columns(own, row, to_east, to_west)
        return carry

    lax.fori_loop(0, RUN, columns_loop, 0)

    @pl.when(has_south)
    def _():
        pl.semaphore_wait(barrier, 4)

    @pl.when(lat == 0)
    def _():
        pl.semaphore_wait(barrier, 3)

    def remote(src, dst, send, recv, at_lon, at_lat):
        return pltpu.make_async_remote_copy(
            src_ref=src, dst_ref=dst, send_sem=send_sem.at[send], recv_sem=recv_sem.at[recv],
            device_id={"lon": at_lon, "lat": at_lat}, device_id_type=MESH,
        )

    southern, northern = f.at[:, pl.ds(0, HALO)], f.at[:, pl.ds(TILE + HALO, HALO)]
    send_north = remote(
        f.at[:, pl.ds(TILE, HALO)], f.at[:, pl.ds(top * (TILE + HALO), HALO)], 0, top, north_lon, north_lat
    )
    send_south = remote(f.at[:, pl.ds(HALO, HALO)], northern, 1, 1, lon, lat - 1)
    from_south = remote(southern, southern, 0, 0, lon, lat)
    from_north = remote(northern, northern, 0, 1, lon, lat)
    send_east = remote(to_east, from_west, 2, 2, right, lat)
    send_west = remote(to_west, from_east, 3, 3, left, lat)
    send_late_east = remote(late_east, late_from_west, 4, 4, right, lat)
    send_late_west = remote(late_west, late_from_east, 5, 5, left, lat)

    send_north.start()

    @pl.when(has_south)
    def _():
        send_south.start()

    send_east.start()
    send_west.start()

    def flux_loop(i, carry):
        flux_row(f, x, 4 + 6 * i, 6)
        return carry

    lax.fori_loop(0, 21, flux_loop, 0)

    from_north.wait_recv()
    send_north.wait_send()

    @pl.when(has_south)
    def _():
        from_south.wait_recv()
        send_south.wait_send()

    @pl.when(is_top)
    def _():
        above = TILE + HALO
        for q in (T, S, WET, U):
            rows = [mirrored(f[q, above + i], lane) for i in (2, 1, 0)]
            for i in range(3):
                f[q, above + i] = -rows[i] if q == U else rows[i]
        rows = [mirrored(f[V, above + i], lane) for i in (2, 1, 0)]
        f[V, above - 1] = 0.5 * (f[V, above - 1] - rows[0])
        f[V, above] = -rows[1]
        f[V, above + 1] = -rows[2]

    for row in range(HALO):
        for q in range(5):
            ahead = TILE + HALO + row - (1 if q == V else 0)
            value = placed(window(f[q, row]), 0, jnp.zeros((LEVELS, 128), jnp.float32))
            late[q, row] = placed(window(f[q, ahead]), LAST, value)
        columns(late, row, late_east, late_west)
    send_late_east.start()
    send_late_west.start()

    @pl.when(is_top)
    def _():
        for i in range(3):
            f[U, TILE + HALO + i] = east(f[U, TILE + HALO + i])

    def flux_rest(i, carry):
        flux_row(f, x, 1 + 126 * i, 6)
        return carry

    lax.fori_loop(0, 2, flux_rest, 0)

    def ratio_loop(i, carry):
        ratio_row(x, r, 2 + 5 * i, 5)
        return carry

    lax.fori_loop(0, 26, ratio_loop, 0)

    send_east.wait()
    send_west.wait()
    send_late_east.wait()
    send_late_west.wait()

    def joined(source, q, row, west_part, east_part):
        value = jnp.where(slot < 3, roll(west_part[row], -3 * q), source[q, row])
        return jnp.where(slot >= 15, roll(east_part[row], 15 - 3 * q), value)

    def join_loop(row, carry):
        for q in range(5):
            e[q, row + HALO] = joined(own, q, row, from_west, from_east)
        return carry

    lax.fori_loop(0, RUN, join_loop, 0)

    for row in range(HALO):
        for q in range(5):
            value = joined(late, q, row, late_from_west, late_from_east)
            late[q, row] = value
            at = HALO + TAIL + row - (1 if q == V else 0)
            e[q, at] = jnp.where(group == LAST, value, e[q, at])

    @pl.when(is_top)
    def _():
        for row in range(HALO):
            at = HALO + TAIL + row
            e[U, at] = jnp.where(group == LAST, east(e[U, at]), e[U, at])

    for row in range(HALO):
        for q in range(5):
            e[q, row] = jnp.where(group == 0, late[q, row], roll(e[q, RUN + row], SPAN))
            e[q, RUN + HALO + row] = roll(e[q, HALO + row], -SPAN)

    def edge_flux(i, carry):
        flux_row(e, xe, 1 + 6 * i, 6)
        return carry

    lax.fori_loop(0, 4, edge_flux, 0)

    def edge_ratio(i, carry):
        ratio_row(xe, re, 2 + 2 * i, 2)
        return carry

    lax.fori_loop(0, 11, edge_ratio, 0)

    def edge_final(i, carry):
        def emit(n, k, value):
            eq[n, 4 * i + k] = value

        final_row(xe, re, HALO + 4 * i, 4, emit)
        return carry

    lax.fori_loop(0, 5, edge_final, 0)

    def final_loop(i, carry):
        g = i // 5
        shift_w = lax.rem(128 - HALO - g * SPAN + 128, 128)
        shift_e = lax.rem(113 - g * SPAN + 128, 128)

        def emit(n, k, value):
            j = 4 * i + k
            edge = eq[n, j - g * RUN]
            value = jnp.where(lane < 3, pltpu.roll(edge, shift_w, 1), value)
            value = jnp.where(lane >= 125, pltpu.roll(edge, shift_e, 1), value)
            result[n, pl.ds(j, 8, stride=TILE), :] = value[:8]
            result[n, pl.ds(j + 8 * TILE, 8, stride=TILE), :] = value[8:]

        final_row(x, r, HALO + 4 * i, 4, emit)
        return carry

    lax.fori_loop(0, 32, final_loop, 0)

    stores = [
        pltpu.make_async_copy(result.at[n], dst, out_sem.at[n]) for n, dst in enumerate((t_out, s_out))
    ]
    for copy in stores:
        copy.start()
    for copy in stores:
        copy.wait()


def solution(mesh):
    lons, lats = mesh.shape["lon"], mesh.shape["lat"]

    def step(t, s, u, v, ind, tally):
        flat = (LEVELS * TILE, TILE)
        vector = (LEVELS, 128)
        vmem = lambda *shape: pltpu.VMEM(shape, jnp.float32)
        outs = pl.pallas_call(
            functools.partial(kernel, lons, lats),
            out_shape=[jax.ShapeDtypeStruct(flat, jnp.float32)] * 2,
            in_specs=[pl.BlockSpec(memory_space=pl.ANY)] * 6,
            out_specs=[pl.BlockSpec(memory_space=pl.ANY)] * 2,
            scratch_shapes=[
                vmem(4, *flat),
                pltpu.VMEM(flat, jnp.int32),
                pltpu.VMEM((TILE, TILE), jnp.int32),
                vmem(5, ROWS, *vector),
                vmem(7, 2, ROWS, *vector),
                vmem(2, 2, ROWS, *vector),
                vmem(5, EDGE_ROWS, *vector),
                vmem(7, 2, EDGE_ROWS, *vector),
                vmem(2, 2, EDGE_ROWS, *vector),
                vmem(2, RUN, *vector),
                vmem(5, RUN, *vector),
                vmem(5, HALO, *vector),
                *[vmem(RUN, *vector)] * 4,
                *[vmem(HALO, *vector)] * 4,
                vmem(2, *flat),
                pltpu.SemaphoreType.DMA((6,)),
                pltpu.SemaphoreType.DMA((2,)),
                pltpu.SemaphoreType.DMA((6,)),
                pltpu.SemaphoreType.DMA((6,)),
            ],
            compiler_params=pltpu.CompilerParams(
                collective_id=0, has_side_effects=True, vmem_limit_bytes=60 * 1024 * 1024
            ),
        )(t.reshape(flat), s.reshape(flat), u.reshape(flat), v.reshape(flat), ind.reshape(flat), tally)
        return tuple(out.reshape(LEVELS, TILE, TILE) for out in outs)

    spec = P(None, "lat", "lon")
    return jax.shard_map(
        step,
        mesh=mesh,
        in_specs=(spec,) * 5 + (P("lat", "lon"),),
        out_specs=(spec, spec),
        check_vma=False,
    )
```

```python
import functools

import jax
import jax.numpy as jnp
from jax import lax
from jax.experimental import pallas as pl
from jax.experimental.pallas import tpu as pltpu
from jax.sharding import PartitionSpec as P

MESH = pl.DeviceIdType.MESH
DIFFUSIVITY = 0.12
LIMIT_FLOOR = 0.01
BIG = 1e30

LEVELS = 16
TILE = 128
HALO = 3
ROWS = TILE + 2 * HALO
SPAN = 18
GROUPS = 7
RUN = 20
EDGE_ROWS = RUN + 2 * HALO
LAST = GROUPS - 1
FLUX_ROWS, RATIO_ROWS, FINAL_ROWS = 6, 5, 8
EDGE_FLUX, EDGE_RATIO, EDGE_FINAL = 6, 11, 10
PART = 32
TAIL = TILE - LAST * RUN

T, S, U, V, WET = range(5)
UP, LO, AX, AY, LOW, DX, DY = range(7)


def roll(value, shift):
    return pltpu.roll(value, shift % 128, 1)


def east(value):
    return roll(value, -1)


def west(value):
    return roll(value, 1)


def flux_row(f, x, base, count):
    wet = [f[WET, base - 1 + i] for i in range(count + 2)]
    tracers = [[f[q, base - 1 + i] for i in range(count + 2)] for q in (T, S)]
    previous = [None, None]
    for i in range(count + 1):
        row = base - 1 + i
        v_mask = wet[i] * wet[i + 1]
        half_y = 0.5 * f[V, row] * v_mask
        speed_y = jnp.abs(half_y)
        mix_y = DIFFUSIVITY * v_mask
        if i > 0:
            u_mask = wet[i] * east(wet[i])
            half_x = 0.5 * f[U, row] * u_mask
            speed_x = jnp.abs(half_x)
            mix_x = DIFFUSIVITY * u_mask
            sea = wet[i] > 0.0
        for n in range(2):
            q, north = tracers[n][i], tracers[n][i + 1]
            slope_y = north - q
            anti_y = speed_y * slope_y
            low_y = half_y * (north + q) - anti_y
            if i > 0:
                right = east(q)
                slope_x = right - q
                anti_x = speed_x * slope_x
                low_x = half_x * (right + q) - anti_x
                low = q - ((low_x - west(low_x)) + (low_y - previous[n]))
                x[UP, n, row] = jnp.where(sea, jnp.maximum(q, low), -BIG)
                x[LO, n, row] = jnp.where(sea, jnp.minimum(q, low), BIG)
                x[AX, n, row] = anti_x
                x[LOW, n, row] = low
                x[DX, n, row] = mix_x * slope_x
            x[AY, n, row] = anti_y
            x[DY, n, row] = mix_y * slope_y
            previous[n] = low_y


def ratio_row(x, r, base, count):
    for n in range(2):
        anti = x[AY, n, base - 1]
        below_in, below_out = jnp.maximum(anti, 0.0), jnp.minimum(anti, 0.0)
        upper = [x[UP, n, base - 1 + i] for i in range(count + 2)]
        lower = [x[LO, n, base - 1 + i] for i in range(count + 2)]
        for i in range(count):
            row = base + i
            high, least = upper[i + 1], lower[i + 1]
            q_max = jnp.maximum(
                jnp.maximum(jnp.maximum(east(high), west(high)), high),
                jnp.maximum(upper[i], upper[i + 2]),
            )
            q_min = jnp.minimum(
                jnp.minimum(jnp.minimum(east(least), west(least)), least),
                jnp.minimum(lower[i], lower[i + 2]),
            )
            anti_x = x[AX, n, row]
            anti_w = west(anti_x)
            anti_y = x[AY, n, row]
            above_in, above_out = jnp.maximum(anti_y, 0.0), jnp.minimum(anti_y, 0.0)
            inflow = (jnp.maximum(anti_w, 0.0) - jnp.minimum(anti_x, 0.0)) + (below_in - above_out)
            outflow = (jnp.maximum(anti_x, 0.0) - jnp.minimum(anti_w, 0.0)) + (above_in - below_out)
            low = x[LOW, n, row]
            r[0, n, row] = jnp.minimum(1.0, (q_max - low) / jnp.maximum(inflow, LIMIT_FLOOR))
            r[1, n, row] = jnp.minimum(1.0, (low - q_min) / jnp.maximum(outflow, LIMIT_FLOOR))
            below_in, below_out = above_in, above_out


def final_row(x, r, base, count, emit):
    for n in range(2):
        into = [r[0, n, base - 1 + i] for i in range(count + 2)]
        out = [r[1, n, base - 1 + i] for i in range(count + 2)]
        previous = None
        for i in range(count + 1):
            row = base - 1 + i
            anti_y = x[AY, n, row]
            limit_y = jnp.where(
                anti_y >= 0.0, jnp.minimum(into[i + 1], out[i]), jnp.minimum(into[i], out[i + 1])
            )
            flux_y = limit_y * anti_y - x[DY, n, row]
            if i > 0:
                anti_x = x[AX, n, row]
                limit_x = jnp.where(
                    anti_x >= 0.0,
                    jnp.minimum(east(into[i]), out[i]),
                    jnp.minimum(into[i], east(out[i])),
                )
                flux_x = limit_x * anti_x - x[DX, n, row]
                emit(n, i - 1, x[LOW, n, row] - ((flux_x - west(flux_x)) + (flux_y - previous)))
            previous = flux_y


def mirrored(value, lane):
    for bit in (64, 32, 16, 8, 4, 2, 1):
        if bit == 64:
            value = roll(value, 64)
        else:
            value = jnp.where(lax.rem(lane // bit, 2) == 1, roll(value, bit), roll(value, -bit))
    return value


def kernel(
    lons, lats,
    t_in, s_in, u_in, v_in, ind_in, tally_in, t_out, s_out,
    nat_i, nat_t, f, x, r, e, xe, re, eq, own, late,
    to_east, to_west, from_west, from_east, late_east, late_west, late_from_west, late_from_east,
    result, in_sem, out_sem, send_sem, recv_sem,
):
    lon, lat = lax.axis_index("lon"), lax.axis_index("lat")
    top = lat // (lats - 1)
    is_top, has_south = lat == lats - 1, lat > 0
    right, left = lax.rem(lon + 1, lons), lax.rem(lon + lons - 1, lons)
    north_lon = lon + top * (lons - 1 - 2 * lon)
    north_lat = lat + 1 - top

    tally_load = pltpu.make_async_copy(tally_in, nat_t, in_sem.at[5])
    tally_load.start()

    inputs = [(ind_in, nat_i), (t_in, f.at[T, pl.ds(HALO, TILE)]), (s_in, f.at[S, pl.ds(HALO, TILE)])]
    inputs += [(u_in, f.at[U, pl.ds(HALO, TILE)]), (v_in, f.at[V, pl.ds(HALO, TILE)])]
    for i, (src, dst) in enumerate(inputs):
        for k in range(LEVELS):
            pltpu.make_async_copy(src.at[k], dst.at[:, k], in_sem.at[i]).start()

    barrier = pltpu.get_barrier_semaphore()

    def greet(at_lon, at_lat):
        pl.semaphore_signal(barrier, inc=1, device_id={"lon": at_lon, "lat": at_lat}, device_id_type=MESH)

    greet(right, lat)
    greet(left, lat)
    greet(north_lon, north_lat)

    @pl.when(has_south)
    def _():
        greet(lon, lat - 1)

    lane = lax.broadcasted_iota(jnp.int32, (LEVELS, 128), 1)
    level = lax.broadcasted_iota(jnp.int32, (LEVELS, 128), 0)
    group = lane // SPAN
    slot = lane - group * SPAN

    def placed(value, at, into):
        first = at * SPAN + HALO
        return jnp.where((lane >= first) & (lane < first + 12), roll(value, first + 6), into)

    def split(fields, row, store, eastward, westward):
        over, under = jnp.zeros((LEVELS, 128), jnp.float32), jnp.zeros((LEVELS, 128), jnp.float32)
        for q in range(5):
            store[q, row] = jnp.where(slot < 9, roll(fields[q], -6), roll(fields[q], 6))
            mine = (slot >= 3 * q) & (slot < 3 * q + 3)
            over = jnp.where(mine, roll(fields[q], 3 * q - 6), over)
            under = jnp.where(mine, roll(fields[q], 3 * q - 9), under)
        eastward[row] = over
        westward[row] = under

    @pl.when(lat == 0)
    def _():
        f[:, 0:HALO] = jnp.zeros((5, HALO, LEVELS, 128), jnp.float32)

    tally_load.wait()
    for i, (_, dst) in enumerate(inputs):
        pltpu.make_async_copy(dst, dst, in_sem.at[i]).wait()

    def pack(groups, row, carry):
        acc = [jnp.zeros((LEVELS, 128), jnp.float32) for _ in range(5)]
        for g in range(groups):
            j = g * RUN + row
            tally = jnp.broadcast_to(nat_t[pl.ds(j, 1), :], (LEVELS, 128))
            wet = jnp.where((nat_i[j] == 1) & (level < tally), 1.0, 0.0).astype(jnp.float32)
            f[WET, j + HALO] = wet
            for q in range(5):
                acc[q] = placed(wet if q == WET else f[q, j + HALO], g, acc[q])
        split(acc, row, own, to_east, to_west)
        return carry

    lax.fori_loop(0, TAIL, functools.partial(pack, GROUPS), 0)
    lax.fori_loop(TAIL, RUN, functools.partial(pack, GROUPS - 1), 0)

    @pl.when(has_south)
    def _():
        pl.semaphore_wait(barrier, 4)

    @pl.when(lat == 0)
    def _():
        pl.semaphore_wait(barrier, 3)

    def remote(src, dst, send, recv, at_lon, at_lat):
        return pltpu.make_async_remote_copy(
            src_ref=src, dst_ref=dst, send_sem=send_sem.at[send], recv_sem=recv_sem.at[recv],
            device_id={"lon": at_lon, "lat": at_lat}, device_id_type=MESH,
        )

    southern, northern = f.at[:, pl.ds(0, HALO)], f.at[:, pl.ds(TILE + HALO, HALO)]
    send_north = remote(
        f.at[:, pl.ds(TILE, HALO)], f.at[:, pl.ds(top * (TILE + HALO), HALO)], 0, top, north_lon, north_lat
    )
    send_south = remote(f.at[:, pl.ds(HALO, HALO)], northern, 1, 1, lon, lat - 1)
    from_south = remote(southern, southern, 0, 0, lon, lat)
    from_north = remote(northern, northern, 0, 1, lon, lat)
    send_east = remote(to_east, from_west, 2, 2, right, lat)
    send_west = remote(to_west, from_east, 3, 3, left, lat)
    send_late_east = remote(late_east, late_from_west, 4, 4, right, lat)
    send_late_west = remote(late_west, late_from_east, 5, 5, left, lat)

    send_north.start()

    @pl.when(has_south)
    def _():
        send_south.start()

    send_east.start()
    send_west.start()

    def flux_loop(i, carry):
        flux_row(f, x, 4 + FLUX_ROWS * i, FLUX_ROWS)
        return carry

    lax.fori_loop(0, 126 // FLUX_ROWS, flux_loop, 0)

    from_north.wait_recv()
    send_north.wait_send()

    @pl.when(has_south)
    def _():
        from_south.wait_recv()
        send_south.wait_send()

    @pl.when(is_top)
    def _():
        above = TILE + HALO
        for q in (T, S, WET, U):
            rows = [mirrored(f[q, above + i], lane) for i in (2, 1, 0)]
            for i in range(3):
                f[q, above + i] = -rows[i] if q == U else rows[i]
        rows = [mirrored(f[V, above + i], lane) for i in (2, 1, 0)]
        f[V, above - 1] = 0.5 * (f[V, above - 1] - rows[0])
        f[V, above] = -rows[1]
        f[V, above + 1] = -rows[2]

    for row in range(HALO):
        fields = []
        for q in range(5):
            ahead = TILE + HALO + row - (1 if q == V else 0)
            value = placed(f[q, row], 0, jnp.zeros((LEVELS, 128), jnp.float32))
            fields.append(placed(f[q, ahead], LAST, value))
        split(fields, row, late, late_east, late_west)
    send_late_east.start()
    send_late_west.start()

    @pl.when(is_top)
    def _():
        for i in range(3):
            f[U, TILE + HALO + i] = east(f[U, TILE + HALO + i])

    def flux_rest(i, carry):
        flux_row(f, x, 1 + 129 * i, 3)
        return carry

    lax.fori_loop(0, 2, flux_rest, 0)

    def ratio_loop(i, carry):
        ratio_row(x, r, 2 + RATIO_ROWS * i, RATIO_ROWS)
        return carry

    lax.fori_loop(0, 130 // RATIO_ROWS, ratio_loop, 0)

    send_east.wait()
    send_west.wait()
    send_late_east.wait()
    send_late_west.wait()

    def joined(source, q, row, west_part, east_part):
        value = jnp.where(slot < 3, roll(west_part[row], -3 * q), source[q, row])
        return jnp.where(slot >= 15, roll(east_part[row], 15 - 3 * q), value)

    def join_loop(row, carry):
        for q in range(5):
            e[q, row + HALO] = joined(own, q, row, from_west, from_east)
        return carry

    lax.fori_loop(0, RUN, join_loop, 0)

    for row in range(HALO):
        for q in range(5):
            value = joined(late, q, row, late_from_west, late_from_east)
            late[q, row] = value
            at = HALO + TAIL + row - (1 if q == V else 0)
            e[q, at] = jnp.where(group == LAST, value, e[q, at])

    @pl.when(is_top)
    def _():
        for row in range(HALO):
            at = HALO + TAIL + row
            e[U, at] = jnp.where(group == LAST, east(e[U, at]), e[U, at])

    for row in range(HALO):
        for q in range(5):
            e[q, row] = jnp.where(group == 0, late[q, row], roll(e[q, RUN + row], SPAN))
            e[q, RUN + HALO + row] = roll(e[q, HALO + row], -SPAN)

    def edge_flux(i, carry):
        flux_row(e, xe, 1 + EDGE_FLUX * i, EDGE_FLUX)
        return carry

    lax.fori_loop(0, 24 // EDGE_FLUX, edge_flux, 0)

    def edge_ratio(i, carry):
        ratio_row(xe, re, 2 + EDGE_RATIO * i, EDGE_RATIO)
        return carry

    lax.fori_loop(0, 22 // EDGE_RATIO, edge_ratio, 0)

    def edge_final(i, carry):
        def emit(n, k, value):
            eq[n, EDGE_FINAL * i + k] = jnp.where(slot >= 15, roll(value, 12), value)

        final_row(xe, re, HALO + EDGE_FINAL * i, EDGE_FINAL, emit)
        return carry

    lax.fori_loop(0, RUN // EDGE_FINAL, edge_final, 0)

    border = (lane < 3) | (lane >= 125)

    def final_loop(i, carry):
        def emit(n, k, value):
            j = FINAL_ROWS * i + k
            g = j // RUN
            shift = lax.rem(113 - g * SPAN + 128, 128)
            result[n, j] = jnp.where(border, pltpu.roll(eq[n, j - g * RUN], shift, 1), value)

        final_row(x, r, HALO + FINAL_ROWS * i, FINAL_ROWS, emit)
        return carry

    def part_loop(i, carry):
        lax.fori_loop(i * (PART // FINAL_ROWS), (i + 1) * (PART // FINAL_ROWS), final_loop, 0)
        rows = pl.ds(pl.multiple_of(i * PART, PART), PART)
        for n, dst in enumerate((t_out, s_out)):
            for k in range(LEVELS):
                pltpu.make_async_copy(result.at[n, rows, k], dst.at[k, rows], out_sem.at[n]).start()
        return carry

    lax.fori_loop(0, TILE // PART, part_loop, 0)
    for n in range(2):
        pltpu.make_async_copy(result.at[n], result.at[n], out_sem.at[n]).wait()


def solution(mesh):
    lons, lats = mesh.shape["lon"], mesh.shape["lat"]

    def step(t, s, u, v, ind, tally):
        shape = (LEVELS, TILE, TILE)
        vector = (LEVELS, 128)
        vmem = lambda *shape: pltpu.VMEM(shape, jnp.float32)
        outs = pl.pallas_call(
            functools.partial(kernel, lons, lats),
            out_shape=[jax.ShapeDtypeStruct(shape, jnp.float32)] * 2,
            in_specs=[pl.BlockSpec(memory_space=pl.ANY)] * 6,
            out_specs=[pl.BlockSpec(memory_space=pl.ANY)] * 2,
            scratch_shapes=[
                pltpu.VMEM((TILE, *vector), jnp.int32),
                pltpu.VMEM((TILE, TILE), jnp.int32),
                vmem(5, ROWS, *vector),
                vmem(7, 2, ROWS, *vector),
                vmem(2, 2, ROWS, *vector),
                vmem(5, EDGE_ROWS, *vector),
                vmem(7, 2, EDGE_ROWS, *vector),
                vmem(2, 2, EDGE_ROWS, *vector),
                vmem(2, RUN, *vector),
                vmem(5, RUN, *vector),
                vmem(5, HALO, *vector),
                *[vmem(RUN, *vector)] * 4,
                *[vmem(HALO, *vector)] * 4,
                vmem(2, TILE, *vector),
                pltpu.SemaphoreType.DMA((6,)),
                pltpu.SemaphoreType.DMA((2,)),
                pltpu.SemaphoreType.DMA((6,)),
                pltpu.SemaphoreType.DMA((6,)),
            ],
            compiler_params=pltpu.CompilerParams(
                collective_id=0, has_side_effects=True, vmem_limit_bytes=60 * 1024 * 1024
            ),
        )(t, s, u, v, ind, tally)
        return tuple(outs)

    spec = P(None, "lat", "lon")
    return jax.shard_map(
        step,
        mesh=mesh,
        in_specs=(spec,) * 5 + (P("lat", "lon"),),
        out_specs=(spec, spec),
        check_vma=False,
    )
```

```python
import functools

import jax
import jax.numpy as jnp
from jax import lax
from jax.experimental import pallas as pl
from jax.experimental.pallas import tpu as pltpu
from jax.sharding import PartitionSpec as P

MESH = pl.DeviceIdType.MESH
DIFFUSIVITY = 0.12
LIMIT_FLOOR = 0.01
BIG = 1e30

LEVELS = 16
TILE = 128
HALO = 3
ROWS = TILE + 2 * HALO
SPAN = 18
GROUPS = 7
RUN = 20
EDGE_ROWS = RUN + 2 * HALO
LAST = GROUPS - 1
FLUX_ROWS, RATIO_ROWS, FINAL_ROWS = 6, 6, 8
EDGE_FLUX, EDGE_RATIO, EDGE_FINAL = 6, 11, 10
PART = 32
TAIL = TILE - LAST * RUN

T, S, U, V, WET = range(5)
UP, LO, AX, AY, LOW, DX, DY = range(7)


def roll(value, shift):
    return pltpu.roll(value, shift % 128, 1)


def east(value):
    return roll(value, -1)


def west(value):
    return roll(value, 1)


def flux_row(f, x, base, count):
    wet = [f[WET, base - 1 + i] for i in range(count + 2)]
    tracers = [[f[q, base - 1 + i] for i in range(count + 2)] for q in (T, S)]
    previous = [None, None]
    for i in range(count + 1):
        row = base - 1 + i
        v_mask = wet[i] * wet[i + 1]
        half_y = 0.5 * f[V, row] * v_mask
        speed_y = jnp.abs(half_y)
        mix_y = DIFFUSIVITY * v_mask
        if i > 0:
            u_mask = wet[i] * east(wet[i])
            half_x = 0.5 * f[U, row] * u_mask
            speed_x = jnp.abs(half_x)
            mix_x = DIFFUSIVITY * u_mask
            sea = wet[i] > 0.0
        for n in range(2):
            q, north = tracers[n][i], tracers[n][i + 1]
            slope_y = north - q
            anti_y = speed_y * slope_y
            low_y = half_y * (north + q) - anti_y
            if i > 0:
                right = east(q)
                slope_x = right - q
                anti_x = speed_x * slope_x
                low_x = half_x * (right + q) - anti_x
                low = q - ((low_x - west(low_x)) + (low_y - previous[n]))
                x[UP, n, row] = jnp.where(sea, jnp.maximum(q, low), -BIG)
                x[LO, n, row] = jnp.where(sea, jnp.minimum(q, low), BIG)
                x[AX, n, row] = anti_x
                x[LOW, n, row] = low
                x[DX, n, row] = mix_x * slope_x
            x[AY, n, row] = anti_y
            x[DY, n, row] = mix_y * slope_y
            previous[n] = low_y


def ratio_row(x, r, base, count):
    for n in range(2):
        anti = x[AY, n, base - 1]
        below_in, below_out = jnp.maximum(anti, 0.0), jnp.minimum(anti, 0.0)
        upper = [x[UP, n, base - 1 + i] for i in range(count + 2)]
        lower = [x[LO, n, base - 1 + i] for i in range(count + 2)]
        for i in range(count):
            row = base + i
            high, least = upper[i + 1], lower[i + 1]
            q_max = jnp.maximum(
                jnp.maximum(jnp.maximum(east(high), west(high)), high),
                jnp.maximum(upper[i], upper[i + 2]),
            )
            q_min = jnp.minimum(
                jnp.minimum(jnp.minimum(east(least), west(least)), least),
                jnp.minimum(lower[i], lower[i + 2]),
            )
            anti_x = x[AX, n, row]
            anti_w = west(anti_x)
            anti_y = x[AY, n, row]
            above_in, above_out = jnp.maximum(anti_y, 0.0), jnp.minimum(anti_y, 0.0)
            inflow = (jnp.maximum(anti_w, 0.0) - jnp.minimum(anti_x, 0.0)) + (below_in - above_out)
            outflow = (jnp.maximum(anti_x, 0.0) - jnp.minimum(anti_w, 0.0)) + (above_in - below_out)
            low = x[LOW, n, row]
            r[0, n, row] = jnp.minimum(1.0, (q_max - low) / jnp.maximum(inflow, LIMIT_FLOOR))
            r[1, n, row] = jnp.minimum(1.0, (low - q_min) / jnp.maximum(outflow, LIMIT_FLOOR))
            below_in, below_out = above_in, above_out


def final_row(x, r, base, count, emit):
    for n in range(2):
        into = [r[0, n, base - 1 + i] for i in range(count + 2)]
        out = [r[1, n, base - 1 + i] for i in range(count + 2)]
        previous = None
        for i in range(count + 1):
            row = base - 1 + i
            anti_y = x[AY, n, row]
            limit_y = jnp.where(
                anti_y >= 0.0, jnp.minimum(into[i + 1], out[i]), jnp.minimum(into[i], out[i + 1])
            )
            flux_y = limit_y * anti_y - x[DY, n, row]
            if i > 0:
                anti_x = x[AX, n, row]
                limit_x = jnp.where(
                    anti_x >= 0.0,
                    jnp.minimum(east(into[i]), out[i]),
                    jnp.minimum(into[i], east(out[i])),
                )
                flux_x = limit_x * anti_x - x[DX, n, row]
                emit(n, i - 1, x[LOW, n, row] - ((flux_x - west(flux_x)) + (flux_y - previous)))
            previous = flux_y


def mirrored(value, lane):
    for bit in (64, 32, 16, 8, 4, 2, 1):
        if bit == 64:
            value = roll(value, 64)
        else:
            value = jnp.where(lax.rem(lane // bit, 2) == 1, roll(value, bit), roll(value, -bit))
    return value


def kernel(
    lons, lats,
    t_in, s_in, u_in, v_in, ind_in, tally_in, t_out, s_out, e_out,
    nat_i, nat_t, f, x, r, e, xe, re, eq, own, late,
    to_east, to_west, from_west, from_east, late_east, late_west, late_from_west, late_from_east,
    result, in_sem, out_sem, send_sem, recv_sem,
):
    lon, lat = lax.axis_index("lon"), lax.axis_index("lat")
    top = lat // (lats - 1)
    is_top, has_south = lat == lats - 1, lat > 0
    right, left = lax.rem(lon + 1, lons), lax.rem(lon + lons - 1, lons)
    north_lon = lon + top * (lons - 1 - 2 * lon)
    north_lat = lat + 1 - top

    fields = [(t_in, f.at[T, pl.ds(HALO, TILE)]), (s_in, f.at[S, pl.ds(HALO, TILE)])]
    fields += [(u_in, f.at[U, pl.ds(HALO, TILE)]), (v_in, f.at[V, pl.ds(HALO, TILE)]), (ind_in, nat_i)]

    def load_rows(first, last, sem):
        for q, (src, dst) in enumerate(fields):
            for j in range(first, last):
                pltpu.make_async_copy(src.at[:, j], dst.at[j], in_sem.at[sem + (q == WET)]).start()

    def await_rows(first, last, sem):
        rows = f.at[pl.ds(0, WET), pl.ds(first + HALO, last - first)]
        pltpu.make_async_copy(rows, rows, in_sem.at[sem]).wait()
        rows = nat_i.at[pl.ds(first, last - first)]
        pltpu.make_async_copy(rows, rows, in_sem.at[sem + 1]).wait()

    tally_load = pltpu.make_async_copy(tally_in, nat_t, in_sem.at[6])
    tally_load.start()
    load_rows(0, HALO, 0)
    load_rows(TILE - HALO, TILE, 2)
    load_rows(HALO, 8, 4)
    load_rows(TILE - 8, TILE - HALO, 4)
    for q, (src, dst) in enumerate(fields):
        for k in range(LEVELS):
            inner = pl.ds(8, TILE - 16)
            pltpu.make_async_copy(src.at[k, inner], dst.at[inner, k], in_sem.at[4 + (q == WET)]).start()

    barrier = pltpu.get_barrier_semaphore()

    def greet(at_lon, at_lat):
        pl.semaphore_signal(barrier, inc=1, device_id={"lon": at_lon, "lat": at_lat}, device_id_type=MESH)

    greet(right, lat)
    greet(left, lat)
    greet(north_lon, north_lat)

    @pl.when(has_south)
    def _():
        greet(lon, lat - 1)

    lane = lax.broadcasted_iota(jnp.int32, (LEVELS, 128), 1)
    level = lax.broadcasted_iota(jnp.int32, (LEVELS, 128), 0)
    group = lane // SPAN
    slot = lane - group * SPAN

    def placed(value, at, into):
        first = at * SPAN + HALO
        return jnp.where((lane >= first) & (lane < first + 12), roll(value, first + 6), into)

    def split(fields, row, store, eastward, westward):
        over, under = jnp.zeros((LEVELS, 128), jnp.float32), jnp.zeros((LEVELS, 128), jnp.float32)
        for q in range(5):
            store[q, row] = jnp.where(slot < 9, roll(fields[q], -6), roll(fields[q], 6))
            mine = (slot >= 3 * q) & (slot < 3 * q + 3)
            over = jnp.where(mine, roll(fields[q], 3 * q - 6), over)
            under = jnp.where(mine, roll(fields[q], 3 * q - 9), under)
        eastward[row] = over
        westward[row] = under

    @pl.when(lat == 0)
    def _():
        f[:, 0:HALO] = jnp.zeros((5, HALO, LEVELS, 128), jnp.float32)

    def sea_row(j):
        tally = jnp.broadcast_to(nat_t[pl.ds(j, 1), :], (LEVELS, 128))
        return jnp.where((nat_i[j] == 1) & (level < tally), 1.0, 0.0).astype(jnp.float32)

    tally_load.wait()
    await_rows(0, HALO, 0)
    await_rows(TILE - HALO, TILE, 2)
    for j in (*range(HALO), *range(TILE - HALO, TILE)):
        f[WET, j + HALO] = sea_row(j)

    @pl.when(has_south)
    def _():
        pl.semaphore_wait(barrier, 4)

    @pl.when(lat == 0)
    def _():
        pl.semaphore_wait(barrier, 3)

    def remote(src, dst, send, recv, at_lon, at_lat):
        return pltpu.make_async_remote_copy(
            src_ref=src, dst_ref=dst, send_sem=send_sem.at[send], recv_sem=recv_sem.at[recv],
            device_id={"lon": at_lon, "lat": at_lat}, device_id_type=MESH,
        )

    southern, northern = f.at[:, pl.ds(0, HALO)], f.at[:, pl.ds(TILE + HALO, HALO)]
    send_north = remote(
        f.at[:, pl.ds(TILE, HALO)], f.at[:, pl.ds(top * (TILE + HALO), HALO)], 0, top, north_lon, north_lat
    )
    send_south = remote(f.at[:, pl.ds(HALO, HALO)], northern, 1, 1, lon, lat - 1)
    from_south = remote(southern, southern, 0, 0, lon, lat)
    from_north = remote(northern, northern, 0, 1, lon, lat)
    send_east = remote(to_east, from_west, 2, 2, right, lat)
    send_west = remote(to_west, from_east, 3, 3, left, lat)
    send_late_east = remote(late_east, late_from_west, 4, 4, right, lat)
    send_late_west = remote(late_west, late_from_east, 5, 5, left, lat)

    send_north.start()

    @pl.when(has_south)
    def _():
        send_south.start()

    await_rows(HALO, TILE - HALO, 4)

    def pack(groups, kept, row, carry):
        acc = [jnp.zeros((LEVELS, 128), jnp.float32) for _ in range(5)]
        for g in range(groups):
            j = g * RUN + row
            wet = sea_row(j)
            if g != kept:
                f[WET, j + HALO] = wet
            for q in range(5):
                acc[q] = placed(wet if q == WET else f[q, j + HALO], g, acc[q])
        split(acc, row, own, to_east, to_west)
        return carry

    for first, last, groups, kept in (
        (0, HALO, GROUPS, 0),
        (HALO, TAIL - HALO, GROUPS, None),
        (TAIL - HALO, TAIL, GROUPS, LAST),
        (TAIL, RUN, LAST, None),
    ):
        lax.fori_loop(first, last, functools.partial(pack, groups, kept), 0)

    send_east.start()
    send_west.start()

    def flux_loop(i, carry):
        flux_row(f, x, 4 + FLUX_ROWS * i, FLUX_ROWS)
        return carry

    lax.fori_loop(0, 126 // FLUX_ROWS, flux_loop, 0)

    def ratio_loop(i, carry):
        ratio_row(x, r, 5 + RATIO_ROWS * i, RATIO_ROWS)
        return carry

    lax.fori_loop(0, 120 // RATIO_ROWS, ratio_loop, 0)
    ratio_row(x, r, 125, 4)

    from_north.wait_recv()
    send_north.wait_send()

    @pl.when(has_south)
    def _():
        from_south.wait_recv()
        send_south.wait_send()

    @pl.when(is_top)
    def _():
        above = TILE + HALO
        for q in (T, S, WET, U):
            rows = [mirrored(f[q, above + i], lane) for i in (2, 1, 0)]
            for i in range(3):
                f[q, above + i] = -rows[i] if q == U else rows[i]
        rows = [mirrored(f[V, above + i], lane) for i in (2, 1, 0)]
        f[V, above - 1] = 0.5 * (f[V, above - 1] - rows[0])
        f[V, above] = -rows[1]
        f[V, above + 1] = -rows[2]

    for row in range(HALO):
        fields = []
        for q in range(5):
            ahead = TILE + HALO + row - (1 if q == V else 0)
            value = placed(f[q, row], 0, jnp.zeros((LEVELS, 128), jnp.float32))
            fields.append(placed(f[q, ahead], LAST, value))
        split(fields, row, late, late_east, late_west)
    send_late_east.start()
    send_late_west.start()

    @pl.when(is_top)
    def _():
        for i in range(3):
            f[U, TILE + HALO + i] = east(f[U, TILE + HALO + i])

    def emit_at(base, n, k, value):
        result[n, base - HALO + k] = value

    def final_loop(i, carry):
        base = 6 + FINAL_ROWS * i
        final_row(x, r, base, FINAL_ROWS, functools.partial(emit_at, base))
        return carry

    lax.fori_loop(0, 120 // FINAL_ROWS, final_loop, 0)

    def put(n, first, last):
        rows = pl.ds(first, last - first)
        return pltpu.make_async_copy(result.at[n, rows], (t_out, s_out)[n].at[rows], out_sem.at[n])

    for n in range(2):
        put(n, 8, 123).start()

    def flux_rest(i, carry):
        flux_row(f, x, 1 + 129 * i, 3)
        return carry

    lax.fori_loop(0, 2, flux_rest, 0)

    def ratio_rest(i, carry):
        ratio_row(x, r, 2 + 127 * i, 3)
        return carry

    lax.fori_loop(0, 2, ratio_rest, 0)

    def final_rest(i, carry):
        base = HALO + 123 * i
        final_row(x, r, base, 5, functools.partial(emit_at, base))
        return carry

    lax.fori_loop(0, 2, final_rest, 0)

    for n in range(2):
        put(n, 0, 8).start()
        put(n, 123, TILE).start()

    send_east.wait()
    send_west.wait()
    def joined(source, q, row, west_part, east_part):
        value = jnp.where(slot < 3, roll(west_part[row], -3 * q), source[q, row])
        return jnp.where(slot >= 15, roll(east_part[row], 15 - 3 * q), value)

    def join_loop(row, carry):
        for q in range(5):
            e[q, row + HALO] = joined(own, q, row, from_west, from_east)
        return carry

    lax.fori_loop(0, RUN, join_loop, 0)

    send_late_east.wait()
    send_late_west.wait()
    for row in range(HALO):
        for q in range(5):
            value = joined(late, q, row, late_from_west, late_from_east)
            late[q, row] = value
            at = HALO + TAIL + row - (1 if q == V else 0)
            e[q, at] = jnp.where(group == LAST, value, e[q, at])

    @pl.when(is_top)
    def _():
        for row in range(HALO):
            at = HALO + TAIL + row
            e[U, at] = jnp.where(group == LAST, east(e[U, at]), e[U, at])

    for row in range(HALO):
        for q in range(5):
            e[q, row] = jnp.where(group == 0, late[q, row], roll(e[q, RUN + row], SPAN))
            e[q, RUN + HALO + row] = roll(e[q, HALO + row], -SPAN)

    def edge_flux(i, carry):
        flux_row(e, xe, 1 + EDGE_FLUX * i, EDGE_FLUX)
        return carry

    lax.fori_loop(0, 24 // EDGE_FLUX, edge_flux, 0)

    def edge_ratio(i, carry):
        ratio_row(xe, re, 2 + EDGE_RATIO * i, EDGE_RATIO)
        return carry

    lax.fori_loop(0, 22 // EDGE_RATIO, edge_ratio, 0)

    def edge_final(i, carry):
        def emit(n, k, value):
            eq[n, EDGE_FINAL * i + k] = jnp.where(slot >= 15, roll(value, 12), value)

        final_row(xe, re, HALO + EDGE_FINAL * i, EDGE_FINAL, emit)
        return carry

    lax.fori_loop(0, RUN // EDGE_FINAL, edge_final, 0)

    put_edges = pltpu.make_async_copy(eq, e_out, out_sem.at[2])
    put_edges.start()
    for n in range(2):
        rows = result.at[n]
        pltpu.make_async_copy(rows, rows, out_sem.at[n]).wait()
    put_edges.wait()


def finish(t_in, s_in, e_in, t_out, s_out, eq, result, in_sem, out_sem):
    edges = pltpu.make_async_copy(e_in, eq, in_sem.at[0])
    edges.start()

    def load(n, part):
        rows = pl.ds(part * PART, PART)
        return pltpu.make_async_copy((t_in, s_in)[n].at[rows], result.at[n, rows], in_sem.at[1 + n * (TILE // PART) + part])

    for part in range(TILE // PART):
        for n in range(2):
            load(n, part).start()
    lane = lax.broadcasted_iota(jnp.int32, (LEVELS, 128), 1)
    border = (lane < 3) | (lane >= 125)

    def patch(i, carry):
        for n in range(2):
            for k in range(FINAL_ROWS):
                j = FINAL_ROWS * i + k
                g = j // RUN
                shift = lax.rem(113 - g * SPAN + 128, 128)
                result[n, j] = jnp.where(border, pltpu.roll(eq[n, j - g * RUN], shift, 1), result[n, j])
        return carry

    edges.wait()
    for part in range(TILE // PART):
        for n in range(2):
            load(n, part).wait()
        lax.fori_loop(part * (PART // FINAL_ROWS), (part + 1) * (PART // FINAL_ROWS), patch, 0)
        rows = pl.ds(part * PART, PART)
        for n, dst in enumerate((t_out, s_out)):
            for k in range(LEVELS):
                pltpu.make_async_copy(result.at[n, rows, k], dst.at[k, rows], out_sem.at[n]).start()
    for n in range(2):
        pltpu.make_async_copy(result.at[n], result.at[n], out_sem.at[n]).wait()


def solution(mesh):
    lons, lats = mesh.shape["lon"], mesh.shape["lat"]

    def step(t, s, u, v, ind, tally):
        shape = (LEVELS, TILE, TILE)
        vector = (LEVELS, 128)
        vmem = lambda *shape: pltpu.VMEM(shape, jnp.float32)
        outs = pl.pallas_call(
            functools.partial(kernel, lons, lats),
            out_shape=[jax.ShapeDtypeStruct((TILE, *vector), jnp.float32)] * 2
            + [jax.ShapeDtypeStruct((2, RUN, *vector), jnp.float32)],
            in_specs=[pl.BlockSpec(memory_space=pl.ANY)] * 6,
            out_specs=[pl.BlockSpec(memory_space=pl.ANY)] * 3,
            scratch_shapes=[
                pltpu.VMEM((TILE, *vector), jnp.int32),
                pltpu.VMEM((TILE, TILE), jnp.int32),
                vmem(5, ROWS, *vector),
                vmem(7, 2, ROWS, *vector),
                vmem(2, 2, ROWS, *vector),
                vmem(5, EDGE_ROWS, *vector),
                vmem(7, 2, EDGE_ROWS, *vector),
                vmem(2, 2, EDGE_ROWS, *vector),
                vmem(2, RUN, *vector),
                vmem(5, RUN, *vector),
                vmem(5, HALO, *vector),
                *[vmem(RUN, *vector)] * 4,
                *[vmem(HALO, *vector)] * 4,
                vmem(2, TILE, *vector),
                pltpu.SemaphoreType.DMA((7,)),
                pltpu.SemaphoreType.DMA((3,)),
                pltpu.SemaphoreType.DMA((6,)),
                pltpu.SemaphoreType.DMA((6,)),
            ],
            compiler_params=pltpu.CompilerParams(
                collective_id=0, has_side_effects=True, vmem_limit_bytes=60 * 1024 * 1024
            ),
        )(t, s, u, v, ind, tally)
        return tuple(
            pl.pallas_call(
                finish,
                out_shape=[jax.ShapeDtypeStruct(shape, jnp.float32)] * 2,
                in_specs=[pl.BlockSpec(memory_space=pl.ANY)] * 3,
                out_specs=[pl.BlockSpec(memory_space=pl.ANY)] * 2,
                scratch_shapes=[
                    vmem(2, RUN, *vector),
                    vmem(2, TILE, *vector),
                    pltpu.SemaphoreType.DMA((1 + 2 * TILE // PART,)),
                    pltpu.SemaphoreType.DMA((2,)),
                ],
                compiler_params=pltpu.CompilerParams(vmem_limit_bytes=60 * 1024 * 1024),
            )(*outs)
        )

    spec = P(None, "lat", "lon")
    return jax.shard_map(
        step,
        mesh=mesh,
        in_specs=(spec,) * 5 + (P("lat", "lon"),),
        out_specs=(spec, spec),
        check_vma=False,
    )
```
